32 devices in a mesh: row: 8 (over z, y), col: 4 (over x, core).
Axes of the slice: x: 2, y: 2, z: 4, core: 2. Of those that a mesh axis runs over, the one named last changes fastest.
Arguments:
- jacobian: float32 [16384, 16384], P('row', 'col'), may hold values from -6 to 6
- diff_inputs: float32 [32768, 128], P('row'), may hold values from -0.00390625 to 0.00390625
- diff_outputs: float32 [32768, 128], P('row'), may hold values from -6 to 6
- face_dof: int32 [32768], P('row'), may hold values from 0 to 16383, as said below
- counts: int32 [8], P('row'), may hold values from 128 to 4096, as said below
- residual: float32 [16384], P('col'), may hold values from -0.046875 to 0.046875
- trial: float32 [16384], P('row'), may hold values from -6 to 6
Outputs:
- updated: float32 [16384, 16384], P('row', 'col')
- corrected: float32 [16384], P('row')
The draws below stay inside these ranges and needn't reach their ends.
Inputs may be any that keep to these rules, and one draw needn't show every extreme that they name: Each owner's count is a multiple of 128; the counts sum to 16384; some owner holds exactly 4096. `face_dof`: live slots name every degree of freedom exactly once over all owners, in runs of 128 consecutive degrees of freedom starting at multiples of 128; slots at or past an owner's count hold arbitrary values that belong to no column.
All inputs are finite; a program needn't handle non-finite values. Where the reference program divides by a largest or mean magnitude, that divisor is 1e-20 or more.
Results may differ from the reference program's by a relative error of at most 0.0001.
Values sent between devices are 32-bit elements; how exact they have to be, the bound alone decides.
A program may use at most 192 MiB of HBM per device.

```python
import jax
import jax.numpy as jnp
from jax import lax

M = 16384
K = 128
UNIT = 128
NS = 4
CAP = 4096
N_ROW = 8


def owner_layout(key):
    base = jax.random.fold_in(key, 7)
    key_big, key_fill, key_perm, key_junk = jax.random.split(base, 4)
    units_total = M // UNIT
    most_units = 2 * (units_total // N_ROW)
    biggest = jax.random.randint(key_big, (), 0, N_ROW)
    units = jnp.ones((N_ROW,), jnp.int32).at[biggest].set(most_units)
    remain = units_total - N_ROW - (most_units - 1)

    def add_unit(index, units_now):
        scores = jax.random.randint(jax.random.fold_in(key_fill, index), (N_ROW,), 0, 1 << 20) * N_ROW
        scores = scores + jnp.arange(N_ROW, dtype=jnp.int32)
        scores = jnp.where(units_now >= most_units, -1, scores)
        return units_now.at[jnp.argmax(scores)].add(1)
    units = lax.fori_loop(0, remain, add_unit, units)
    order = jax.random.permutation(key_perm, units_total).astype(jnp.int32)
    starts = jnp.cumsum(units) - units
    slots = jnp.arange(CAP, dtype=jnp.int32)
    live = slots[None, :] < (units * UNIT)[:, None]
    block_index = jnp.clip(starts[:, None] + slots[None, :] // UNIT, 0, units_total - 1)
    dofs = order[block_index] * UNIT + slots[None, :] % UNIT
    junk = jax.random.randint(key_junk, (N_ROW, CAP), 0, M)
    mapped = jnp.where(live, dofs, junk).reshape(-1).astype(jnp.int32)
    return ((units * UNIT).astype(jnp.int32), mapped)


def draw_counts(key, part):
    return owner_layout(key)[0]


def draw_face_dof(key, part):
    return owner_layout(key)[1]


def levels(rng, shape, cuts, smallest, top_value):
    gain, own = 1.0, jax.random.fold_in(rng, 6)
    for dim, blocks in cuts:
        steps = jnp.exp(jax.random.uniform(jax.random.fold_in(own, dim), (blocks,), jnp.float32, smallest / len(cuts), top_value / len(cuts)))
        gain = gain * jnp.repeat(steps, shape[dim] // blocks).reshape([-1 if axis == dim else 1 for axis in range(len(shape))])
    return gain


def gaussian(key, dims, spread, limit, cuts=(), held_as=jnp.bfloat16):
    array = jax.random.normal(key, dims, jnp.float32) * spread
    if len(cuts) > 0:
        array = levels(key, dims, cuts, -0.22, 0.18) * array
    return jnp.clip(array, min=-limit, max=limit).astype(held_as)


def setup_inputs(seed: int = 0) -> dict:
    seeds = jax.random.split(jax.random.key(seed), 8)
    return {
        "jacobian": gaussian(seeds[0], (M, M), 1.0, 6.0, ((0, 8), (1, 4)), jnp.float32),
        "diff_inputs": gaussian(seeds[1], (N_ROW * CAP, K), (M * M // K) ** -0.5, 0.00390625, ((0, 8),), jnp.float32),
        "diff_outputs": gaussian(seeds[2], (N_ROW * CAP, K), 1.0, 6.0, ((0, 8),), jnp.float32),
        "face_dof": draw_face_dof(jax.random.fold_in(seeds[7], 71), 0),
        "counts": draw_counts(jax.random.fold_in(seeds[7], 71), 0),
        "residual": gaussian(seeds[5], (M,), M ** -0.5, 0.046875, ((0, 4),), jnp.float32),
        "trial": gaussian(seeds[6], (M,), 1.0, 6.0, ((0, 8),), jnp.float32),
    }


HIGH = lax.Precision.HIGHEST
REG = 0.1


def ns_inverse(gram):
    eye = jnp.eye(K, dtype=jnp.float32)
    regular = gram + REG * (jnp.trace(gram) / K) * eye
    norm_one = jnp.max(jnp.sum(jnp.abs(regular), axis=0))
    iterate = regular / (norm_one * norm_one)
    for sweep in range(NS):
        iterate = jnp.dot(iterate, 2.0 * eye - jnp.dot(regular, iterate, precision=HIGH), precision=HIGH)
    return iterate


def reference(jacobian, diff_inputs, diff_outputs, face_dof, counts, residual, trial):
    slots = jnp.arange(N_ROW * CAP, dtype=jnp.int32)
    owner = slots // CAP
    live = (slots % CAP) < counts[owner]
    masked = jnp.where(live[:, None], diff_inputs, 0.0)
    gram = jnp.dot(masked.T, masked, precision=HIGH)
    target = jnp.where(live, face_dof, M).astype(jnp.int32)
    inverse = jnp.zeros((M + 1,), jnp.int32).at[target].set(slots)[:M]
    v_full = diff_inputs[inverse]
    w_full = diff_outputs[inverse]
    j_times_v = jnp.dot(jacobian, v_full, precision=HIGH)
    diff = w_full - j_times_v
    zmat = ns_inverse(gram)
    updated = jacobian + jnp.dot(jnp.dot(diff, zmat, precision=HIGH), v_full.T, precision=HIGH)
    corrected = trial - jnp.dot(updated, residual, precision=HIGH)
    return updated, corrected
```

```python
import functools

import jax
import jax.numpy as jnp
from jax import lax
from jax.experimental import pallas as pl
from jax.experimental.pallas import tpu as pltpu
from jax.sharding import PartitionSpec as P

K = 128
NS = 4
UNIT = 128
TILE = 256
VMEM_LIMIT = 26 * 2**20

HIGH = lax.Precision.HIGHEST
REG = 0.1
F32 = jnp.float32
BF16 = jnp.bfloat16
MESH = pl.DeviceIdType.MESH
VMEM_SPEC = pl.BlockSpec(memory_space=pltpu.VMEM)
ANY_SPEC = pl.BlockSpec(memory_space=pl.ANY)
SMEM_SPEC = pl.BlockSpec(memory_space=pltpu.SMEM)


def split(x):
    hi = x.astype(BF16)
    return hi, (x - hi.astype(F32)).astype(BF16)


def ring_place(index, n):
    return index // 2 + (index % 2) * (n - 1 - 2 * (index // 2))


def ring_index(place, n):
    side = place // (n // 2)
    level = place + side * (n - 1 - 2 * place)
    return 2 * level + side


def lookup(run_unit, wanted):
    hit = run_unit[None, :] == wanted[:, None]
    src = jnp.sum(jnp.where(hit, jnp.arange(run_unit.shape[0], dtype=jnp.int32)[None, :], 0), axis=1)
    return src.astype(jnp.int32), jnp.any(hit, axis=1).astype(F32)


def gather_kernel(
    n, nc, parts, w_parts, v_src, v_mask, w_src, w_mask, v_hbm, w_hbm, j_hbm, r_ref,
    j_ref, vt_ref, u_ref, beta_ref, jr_ref,
    xv, xw, whole, landed, sent, vb, gram, beta, jv,
    w_land, w_sent, jv_land, jv_sum, jr_all, gb, gb_all,
    load_sem, j_sem, v_send, v_recv, w_send, w_recv,
    jv_send, jv_recv, gb_send, gb_recv, jr_send, jr_recv, u_send, u_recv,
):
    rows, cols = j_ref.shape
    part = whole.shape[1]
    chunk = part * parts
    grain = w_land.shape[3]
    share = jv_land.shape[1]
    strips, j_rows = jr_ref.shape
    me = lax.axis_index("col")
    place = ring_place(lax.axis_index("row"), n)
    right = ring_index((place + 1) % n, n)
    left = ring_index((place + n - 1) % n, n)
    peers = [(me + k) % nc for k in range(1, nc)]

    def load(k):
        return pltpu.make_async_copy((v_hbm, w_hbm)[k], (xv, xw)[k], load_sem.at[k])

    def j_load(at):
        block = pl.ds(pl.multiple_of(at * j_rows, j_rows), j_rows)
        return pltpu.make_async_copy(j_hbm.at[block], j_ref.at[block], j_sem.at[at])

    load(0).start()
    load(1).start()
    for at in range(strips):
        j_load(at).start()

    barrier = pltpu.get_barrier_semaphore()
    for peer in (left, right):
        pl.semaphore_signal(barrier, inc=1, device_id={"row": peer}, device_id_type=MESH)
    for peer in peers:
        pl.semaphore_signal(barrier, inc=1, device_id={"col": peer}, device_id_type=MESH)
    gram[...] = jnp.zeros_like(gram)
    beta[...] = jnp.zeros_like(beta)
    jv[...] = jnp.zeros_like(jv)
    load(0).wait()
    pl.semaphore_wait(barrier, 2 + len(peers))

    def to_row(source, target, send, recv, way):
        return pltpu.make_async_remote_copy(
            src_ref=source, dst_ref=target, send_sem=send, recv_sem=recv,
            device_id={"row": right if way == 0 else left}, device_id_type=MESH,
        )

    def to_col(source, target, send, recv, peer):
        return pltpu.make_async_remote_copy(
            src_ref=source, dst_ref=target, send_sem=send, recv_sem=recv,
            device_id={"col": peer}, device_id_type=MESH,
        )

    order = [(p, way) for p in range(parts) for way in range(2)]

    def granule(way, back, p):
        sign = 1 if way == 0 else -1
        at = (place + 2 * n - sign * back) % n
        return (way * n + at) * parts + p

    def own(at):
        return xv[v_src[at]] * v_mask[at]

    def reduce_copy(step, way, p):
        return to_row(
            sent.at[way, step, p], landed.at[way, step, p],
            v_send.at[way, step, p], v_recv.at[way, step, p], way,
        )

    def spread_copy(step, way, p, at):
        return to_row(
            whole.at[at], whole.at[at], v_send.at[way, step, p], v_recv.at[way, step, p], way
        )

    def w_copy(step, way, p):
        return to_row(
            w_sent.at[way, step, p], w_land.at[way, step, p],
            w_send.at[way, step, p], w_recv.at[way, step, p], way,
        )

    def w_own(step, way, p):
        sign = 1 if way == 0 else -1
        block = ring_index((place + 2 * n - sign * (step + 1)) % n, n)
        at = (block * 2 + way) * w_parts + p
        return xw[w_src[at]] * w_mask[at]

    def times_residual(at):
        j_load(at).wait()
        strip = min(64, j_rows)
        sums = []
        for sub in range(j_rows // strip):
            block = pl.ds(pl.multiple_of(at * j_rows + sub * strip, strip), strip)
            total = jnp.zeros((strip, K), F32)
            for c in range(0, cols, K):
                total = total + j_ref[block, c : c + K] * r_ref[:, c : c + K]
            sums.append(total)
        total = jnp.concatenate(sums, axis=0)
        jr_all[me, pl.ds(at, 1), :] = jnp.sum(jnp.transpose(total), axis=0, keepdims=True)

    def absorb(block, off, width):
        at = pl.ds(pl.multiple_of(off, width), width)
        hi, lo = split(block)
        both = jnp.concatenate([hi, lo], axis=1)
        vb[at, :] = both
        t_hi, t_lo = split(jnp.transpose(block))
        vt_ref[:K, at] = t_hi
        vt_ref[K:, at] = t_lo
        gram[...] += lax.dot_general(
            both, both, (((0,), (0,)), ((), ())), preferred_element_type=F32
        )
        r_hi, r_lo = split(jnp.broadcast_to(r_ref[:, at], (8, width)))
        beta[...] += jnp.dot(
            jnp.concatenate([r_hi, r_lo], axis=0), both, preferred_element_type=F32
        )

    def accumulate(off, width, first, count):
        tile = min(TILE, count)
        at = pl.ds(pl.multiple_of(off, width), width)

        def body(t, carry):
            block = pl.ds(pl.multiple_of(first + t * tile, tile), tile)
            hi, lo = split(j_ref[block, at])
            both = jnp.dot(
                jnp.concatenate([hi, lo], axis=0), vb[at, :], preferred_element_type=F32
            )
            jv[block, :] += both[:tile, :K] + (both[:tile, K:] + both[tile:, :K]) + both[tile:, K:]
            return carry

        lax.fori_loop(0, count // tile, body, 0)

    piped = chunk % UNIT == 0

    def work(step, p, way):
        if not piped:
            return
        off = granule(way, step, 0) * part
        if p == 0:
            first = pl.multiple_of(granule(way, step, 0), parts)
            absorb(whole[pl.ds(first, parts)].reshape(chunk, K), off, chunk)
        accumulate(off, chunk, p * (rows // parts), rows // parts)

    for p, way in order:
        sent[way, 0, p] = own(granule(way, 0, p))
        reduce_copy(0, way, p).start()
    times_residual(0)

    def reduce_step(step, carry):
        for p, way in order:
            reduce_copy(step - 1, way, p).wait_recv()
            sent[way, step, p] = own(granule(way, step, p)) + landed[way, step - 1, p]
            reduce_copy(step, way, p).start()
        if strips < n - 1:
            pl.when(step < strips)(lambda: times_residual(step))
        else:
            times_residual(step)
        return carry

    lax.fori_loop(1, n - 1, reduce_step, 0)

    for p, way in order:
        reduce_copy(n - 2, way, p).wait_recv()
        at = granule(way, n - 1, p)
        whole[at] = own(at) + landed[way, n - 2, p]
        spread_copy(n - 1, way, p, at).start()
    for at in range(n - 1, strips):
        times_residual(at)

    def jr_copy(k, slot):
        return to_col(jr_all.at[slot], jr_all.at[slot], jr_send.at[k], jr_recv.at[slot], peers[k])

    for k in range(nc - 1):
        jr_copy(k, me).start()

    def spread_step(step, carry):
        for p, way in order:
            at = granule(way, step, p)
            spread_copy(step - 1, way, p, at).wait_recv()
            spread_copy(step, way, p, at).start()
            work(step - 1, p, way)
        return carry

    last = 2 * (n - 1)
    lax.fori_loop(n, last, spread_step, 0)

    w_order = [(p, way) for p in range(w_parts) for way in range(2)]
    load(1).wait()
    for p, way in w_order:
        w_sent[way, 0, p] = w_own(0, way, p)
        w_copy(0, way, p).start()

    for p, way in order:
        spread_copy(last - 1, way, p, granule(way, last, p)).wait_recv()
        work(last - 1, p, way)
    for p, way in order:
        work(last, p, way)
    if not piped:
        per_unit = UNIT // part
        for unit in range(cols // UNIT):
            block = jnp.concatenate([whole[unit * per_unit + s] for s in range(per_unit)], axis=0)
            absorb(block, unit * UNIT, UNIT)
        for off in range(0, cols, 2 * UNIT):
            accumulate(off, 2 * UNIT, 0, rows)

    gb[:K, :] = gram[:K, :K] + (gram[:K, K:] + gram[K:, :K]) + gram[K:, K:]
    gb[K:, :] = beta[:8, :K] + (beta[:8, K:] + beta[8:, :K])

    def gb_copy(k, slot):
        return to_col(gb, gb_all.at[slot], gb_send.at[k], gb_recv.at[slot], peers[k])

    def jv_copy(k, slot, owner):
        block = pl.ds(pl.multiple_of(owner * share, share), share)
        return to_col(jv.at[block], jv_land.at[slot], jv_send.at[k], jv_recv.at[slot], peers[k])

    for k in range(nc - 1):
        gb_copy(k, me).start()
    for k in range(nc - 1):
        jv_copy(k, me, peers[k]).start()

    def w_step(step):
        for p, way in w_order:
            w_copy(step - 1, way, p).wait_recv()
            w_sent[way, step, p] = w_own(step, way, p) + w_land[way, step - 1, p]
            w_copy(step, way, p).start()

    def regularise():
        for k in range(nc - 1):
            gb_copy(k, peers[k]).wait_recv()
        gb_all[me] = gb[...]
        sums = gb_all[0]
        for slot in range(1, nc):
            sums = sums + gb_all[slot]
        beta_ref[...] = sums[K:]
        total = sums[:K]
        trace = jnp.sum(jnp.sum(total * eye, axis=0, keepdims=True), axis=1, keepdims=True)
        regular = total + REG * (trace / K) * eye
        norm_one = jnp.max(
            jnp.sum(jnp.abs(regular), axis=0, keepdims=True), axis=1, keepdims=True
        )
        return regular, regular / (norm_one * norm_one)

    eye = (
        lax.broadcasted_iota(jnp.int32, (K, K), 0) == lax.broadcasted_iota(jnp.int32, (K, K), 1)
    ).astype(F32)
    begin = min(2, n - 2)
    for step in range(1, n - 1):
        w_step(step)
        if step == begin:
            regular, zmat = regularise()
            sweeps = 0
        if step >= begin:
            until = NS if step == n - 2 else min(NS, step - begin + 1)
            for sweep in range(sweeps, until):
                inner = jnp.dot(regular, zmat, precision=HIGH, preferred_element_type=F32)
                zmat = jnp.dot(
                    zmat, 2.0 * eye - inner, precision=HIGH, preferred_element_type=F32
                )
            sweeps = until

    for k in range(nc - 1):
        jv_copy(k, peers[k], me).wait_recv()
    jv_land[me] = jv[pl.ds(pl.multiple_of(me * share, share), share), :]
    total = jv_land[0]
    for slot in range(1, nc):
        total = total + jv_land[slot]
    jv_sum[...] = total

    for k in range(nc - 1):
        jr_copy(k, peers[k]).wait_recv()
    jr_sum = jr_all[0]
    for slot in range(1, nc):
        jr_sum = jr_sum + jr_all[slot]
    jr_ref[...] = jr_sum

    partner = me + 1 - 2 * (me % 2)
    half = nc // 2

    def u_copy(slot, hop, at, peer):
        block = u_ref.at[slot, pl.ds(at * grain, grain)]
        return to_col(block, block, u_send.at[hop, at], u_recv.at[slot, at], peer)

    for p, way in w_order:
        at = way * w_parts + p
        block = pl.ds(at * grain, grain)
        w_copy(n - 2, way, p).wait_recv()
        value = w_own(n - 1, way, p) + w_land[way, n - 2, p]
        u_ref[me, block] = jnp.dot(
            value - jv_sum[block, :], zmat, precision=HIGH, preferred_element_type=F32
        )
        for k in range(1, half):
            u_copy(me, k - 1, at, (me + 2 * k) % nc).start()
        u_copy(me, half - 1, at, partner).start()
    for p, way in w_order:
        at = way * w_parts + p
        for k in range(1, half):
            slot = (me + 2 * k) % nc
            u_copy(slot, half - 1 + k, at, partner).wait_recv()
            u_copy(slot, half - 1 + k, at, partner).start()
    for p, way in w_order:
        at = way * w_parts + p
        for k in range(half):
            u_copy((partner + 2 * k) % nc, 0, at, partner).wait_recv()

    for p, way in w_order:
        for hop in range(nc - 1):
            u_copy(me, hop, way * w_parts + p, partner).wait_send()
    for k in range(nc - 1):
        gb_copy(k, me).wait_send()
        jr_copy(k, me).wait_send()
        jv_copy(k, me, peers[k]).wait_send()

    def drain(step, carry):
        for p, way in order:
            reduce_copy(step, way, p).wait_send()
            spread_copy(step + n - 1, way, p, granule(way, 0, p)).wait_send()
        for p, way in w_order:
            w_copy(step, way, p).wait_send()
        return carry

    lax.fori_loop(0, n - 1, drain, 0)


def gather(v_src, v_mask, w_src, w_mask, diff_inputs, diff_outputs, jacobian, residual, n, nc):
    rows, cols = jacobian.shape
    chunk = cols // (2 * n)
    part = min(UNIT, chunk)
    parts = chunk // part
    share = rows // nc
    grain = min(UNIT, share // 2)
    w_parts = share // (2 * grain)
    strips = min(n, rows // UNIT)
    runs = diff_inputs.shape[0]
    dma = pltpu.SemaphoreType.DMA
    v = pltpu.VMEM
    return pl.pallas_call(
        functools.partial(gather_kernel, n, nc, parts, w_parts),
        out_shape=(
            v((rows, cols), F32),
            v((2 * K, cols), BF16),
            v((nc, share, K), F32),
            v((8, K), F32),
            v((strips, rows // strips), F32),
        ),
        in_specs=[SMEM_SPEC] * 4 + [ANY_SPEC] * 3 + [VMEM_SPEC],
        out_specs=(VMEM_SPEC,) * 5,
        scratch_shapes=[
            v((runs // part, part, K), F32),
            v((runs // grain, grain, K), F32),
            v((cols // part, part, K), F32),
            v((2, n - 1, parts, part, K), F32),
            v((2, n - 1, parts, part, K), F32),
            v((cols, 2 * K), BF16),
            v((2 * K, 2 * K), F32),
            v((16, 2 * K), F32),
            v((rows, K), F32),
            v((2, n - 1, w_parts, grain, K), F32),
            v((2, n - 1, w_parts, grain, K), F32),
            v((nc, share, K), F32),
            v((share, K), F32),
            v((nc, strips, rows // strips), F32),
            v((K + 8, K), F32),
            v((nc, K + 8, K), F32),
            dma((2,)), dma((strips,)),
            dma((2, 2 * (n - 1), parts)), dma((2, 2 * (n - 1), parts)),
            dma((2, n - 1, w_parts)), dma((2, n - 1, w_parts)),
            dma((nc - 1,)), dma((nc,)), dma((nc - 1,)), dma((nc,)),
            dma((nc - 1,)), dma((nc,)),
            dma((nc - 1, share // grain)), dma((nc, share // grain)),
        ],
        compiler_params=pltpu.CompilerParams(
            collective_id=0, has_side_effects=True, vmem_limit_bytes=VMEM_LIMIT
        ),
    )(
        v_src, v_mask, w_src, w_mask,
        diff_inputs.reshape(-1, part, K), diff_outputs.reshape(-1, grain, K), jacobian, residual,
    )


def update_kernel(j_ref, vt_ref, u_ref, beta_ref, jr_ref, trial_ref, out_ref, corrected_ref):
    at = pl.program_id(0)
    tile = out_ref.shape[0]
    block = pl.ds(pl.multiple_of(at * tile, tile), tile)
    u = u_ref[block, :]
    hi, lo = split(u)
    twice = jnp.concatenate([hi, hi], axis=1)
    main = jnp.dot(twice, vt_ref[...], preferred_element_type=F32)
    rest = jnp.dot(lo, vt_ref[:K, :], preferred_element_type=F32)
    out_ref[...] = j_ref[block, :] + (main + rest)
    low_rank = jnp.sum(jnp.transpose(u * beta_ref[:1]), axis=0, keepdims=True)
    corrected_ref[...] = trial_ref[...] - (jr_ref[pl.ds(at, 1), :] + low_rank)


def update(jacobian, vt, u, beta, j_r, trial):
    rows, cols = jacobian.shape
    tile = j_r.shape[1]
    row = pl.BlockSpec((1, tile), lambda i: (0, i))
    held = [pltpu.with_memory_space_constraint(x, pltpu.VMEM) for x in (jacobian, vt, u, beta, j_r)]
    return pl.pallas_call(
        update_kernel,
        grid=(rows // tile,),
        out_shape=(
            jax.ShapeDtypeStruct((rows, cols), F32),
            jax.ShapeDtypeStruct((1, rows), F32),
        ),
        in_specs=[VMEM_SPEC] * 5 + [row],
        out_specs=(pl.BlockSpec((tile, cols), lambda i: (i, 0)), row),
        compiler_params=pltpu.CompilerParams(vmem_limit_bytes=VMEM_LIMIT),
    )(*held, trial)


def per_device(jacobian, diff_inputs, diff_outputs, face_dof, counts, residual, trial):
    row_block, col_block = jacobian.shape
    n_row, n_col = lax.axis_size("row"), lax.axis_size("col")
    col_at = lax.axis_index("col")
    runs = face_dof.shape[0] // UNIT
    first = jnp.arange(runs, dtype=jnp.int32) * UNIT
    run_unit = jnp.where(first < counts[0], face_dof.reshape(runs, UNIT)[:, 0] // UNIT, -1)

    part = min(UNIT, col_block // (2 * n_row))
    per_unit = UNIT // part
    granule = jnp.arange(col_block // part, dtype=jnp.int32)
    v_src, v_mask = lookup(run_unit, col_at * (col_block // UNIT) + granule // per_unit)
    v_src = v_src * per_unit + granule % per_unit

    share = row_block // n_col
    grain = min(UNIT, share // 2)
    per_share = share // grain
    piece = jnp.arange(n_row * per_share, dtype=jnp.int32)
    w_row = (piece // per_share) * row_block + col_at * share + (piece % per_share) * grain
    w_src, w_mask = lookup(run_unit, w_row // UNIT)
    w_src = w_src * (UNIT // grain) + (w_row % UNIT) // grain

    held, vt, u, beta, j_r = gather(
        v_src, v_mask, w_src, w_mask, diff_inputs, diff_outputs, jacobian,
        residual.reshape(1, col_block), n_row, n_col,
    )
    updated, corrected = update(
        held, vt, u.reshape(row_block, K), beta, j_r, trial.reshape(1, row_block)
    )
    return (updated, corrected[0])


def solution(mesh):
    placed = (
        P("row", "col"),
        P("row", None),
        P("row", None),
        P("row"),
        P("row"),
        P("col"),
        P("row"),
    )
    return jax.shard_map(
        per_device,
        mesh=mesh,
        in_specs=placed,
        out_specs=(P("row", "col"), P("row")),
        check_vma=False,
    )
```

```python
import functools

import jax
import jax.numpy as jnp
from jax import lax
from jax.experimental import pallas as pl
from jax.experimental.pallas import tpu as pltpu
from jax.sharding import PartitionSpec as P

K = 128
NS = 4
UNIT = 128
PART = 64
TILE = 1024
WIDTH = 256
VMEM_LIMIT = 26 * 2**20

HIGH = lax.Precision.HIGHEST
REG = 0.1
F32 = jnp.float32
BF16 = jnp.bfloat16
MESH = pl.DeviceIdType.MESH
VMEM_SPEC = pl.BlockSpec(memory_space=pltpu.VMEM)
ANY_SPEC = pl.BlockSpec(memory_space=pl.ANY)
SMEM_SPEC = pl.BlockSpec(memory_space=pltpu.SMEM)


def split(x):
    hi = x.astype(BF16)
    return hi, (x - hi.astype(F32)).astype(BF16)


def ring_place(index, n):
    return index // 2 + (index % 2) * (n - 1 - 2 * (index // 2))


def ring_index(place, n):
    side = place // (n // 2)
    level = place + side * (n - 1 - 2 * place)
    return 2 * level + side


def gather_kernel(
    n, nc, parts, w_parts, dof_ref, count_ref, v_hbm, w_hbm, j_hbm, r_ref,
    j_ref, vt_ref, u_ref, beta_ref, jr_ref,
    run_unit, xv, xw, whole, landed, sent, vb, gram, beta, jv,
    w_land, w_sent, jv_land, jv_sum, jr_all, gb, gb_all,
    load_sem, j_sem, v_send, v_recv, w_send, w_recv,
    jv_send, jv_recv, gb_send, gb_recv, jr_send, jr_recv, u_send, u_recv,
):
    rows, cols = j_ref.shape
    part = whole.shape[1]
    chunk = part * parts
    grain = w_land.shape[3]
    share = jv_land.shape[1]
    strips, j_rows = jr_ref.shape
    me = lax.axis_index("col")
    place = ring_place(lax.axis_index("row"), n)
    right = ring_index((place + 1) % n, n)
    left = ring_index((place + n - 1) % n, n)
    peers = [(me + k) % nc for k in range(1, nc)]

    def load(k):
        return pltpu.make_async_copy((v_hbm, w_hbm)[k], (xv, xw)[k], load_sem.at[k])

    pieces = 2 * parts

    def j_load(at, piece=0, count=1):
        size = j_rows // count
        block = pl.ds(pl.multiple_of(at * j_rows + piece * size, size), size)
        return pltpu.make_async_copy(j_hbm.at[block], j_ref.at[block], j_sem.at[at])

    load(0).start()
    j_load(0).start()

    barrier = pltpu.get_barrier_semaphore()
    for peer in (left, right):
        pl.semaphore_signal(barrier, inc=1, device_id={"row": peer}, device_id_type=MESH)
    for peer in peers:
        pl.semaphore_signal(barrier, inc=1, device_id={"col": peer}, device_id_type=MESH)
    runs = run_unit.shape[0]
    for at in range(runs):
        unit = lax.shift_right_logical(dof_ref[at * UNIT], UNIT.bit_length() - 1)
        run_unit[at] = jnp.where(at * UNIT < count_ref[0], unit, -1)
    load(0).wait()
    pl.semaphore_wait(barrier, 2 + len(peers))

    def to_row(source, target, send, recv, way):
        return pltpu.make_async_remote_copy(
            src_ref=source, dst_ref=target, send_sem=send, recv_sem=recv,
            device_id={"row": right if way == 0 else left}, device_id_type=MESH,
        )

    def to_col(source, target, send, recv, peer):
        return pltpu.make_async_remote_copy(
            src_ref=source, dst_ref=target, send_sem=send, recv_sem=recv,
            device_id={"col": peer}, device_id_type=MESH,
        )

    order = [(p, way) for p in range(parts) for way in range(2)]

    def granule(way, back, p):
        sign = 1 if way == 0 else -1
        at = (place + 2 * n - sign * back) % n
        return (way * n + at) * parts + p

    def locate(unit):
        src = jnp.int32(-1)
        for at in range(runs):
            src = jnp.where(run_unit[at] == unit, at, src)
        return jnp.maximum(src, 0), (src >= 0).astype(F32)

    def pick(source, rows_at):
        size = source.shape[1]
        per_unit = UNIT // size
        found, values = {}, []
        for at, same in rows_at:
            if same is None or same not in found:
                found[same] = locate(at // per_unit)
            src, mask = found[same]
            values.append(lambda src=src, mask=mask, at=at: source[src * per_unit + at % per_unit] * mask)
        return values

    def sharing(p, way, count, size):
        per_unit = UNIT // size
        return (way, p // per_unit) if count % per_unit == 0 else None

    def own(step):
        base = me * (cols // part)
        return pick(
            xv, [(base + granule(way, step, p), sharing(p, way, parts, part)) for p, way in order]
        )

    def reduce_copy(step, way, p):
        return to_row(
            sent.at[way, step, p], landed.at[way, step, p],
            v_send.at[way, step, p], v_recv.at[way, step, p], way,
        )

    def spread_copy(step, way, p, at):
        return to_row(
            whole.at[at], whole.at[at], v_send.at[way, step, p], v_recv.at[way, step, p], way
        )

    def w_copy(step, way, p):
        return to_row(
            w_sent.at[way, step, p], w_land.at[way, step, p],
            w_send.at[way, step, p], w_recv.at[way, step, p], way,
        )

    w_order = [(p, way) for p in range(w_parts) for way in range(2)]

    def w_own(step):
        wanted = []
        for p, way in w_order:
            sign = 1 if way == 0 else -1
            block = ring_index((place + 2 * n - sign * (step + 1)) % n, n)
            at = (block * rows + me * share) // grain + way * w_parts + p
            wanted.append((at, sharing(p, way, w_parts, grain)))
        return pick(xw, wanted)

    def times_residual(at):
        j_load(at).wait()
        strip = min(64, j_rows)
        sums = []
        for sub in range(j_rows // strip):
            block = pl.ds(pl.multiple_of(at * j_rows + sub * strip, strip), strip)
            total = jnp.zeros((strip, K), F32)
            for c in range(0, cols, K):
                total = total + j_ref[block, c : c + K] * r_ref[:, c : c + K]
            sums.append(total)
        total = jnp.concatenate(sums, axis=0)
        jr_all[me, pl.ds(at, 1), :] = jnp.sum(jnp.transpose(total), axis=0, keepdims=True)

    def absorb(block, off, width):
        at = pl.ds(pl.multiple_of(off, width), width)
        hi, lo = split(block)
        both = jnp.concatenate([hi, lo], axis=1)
        vb[at, :] = both
        t_hi, t_lo = split(jnp.transpose(block))
        vt_ref[:K, at] = t_hi
        vt_ref[K:, at] = t_lo
        gram[...] += lax.dot_general(
            both, both, (((0,), (0,)), ((), ())), preferred_element_type=F32
        )
        r_hi, r_lo = split(jnp.broadcast_to(r_ref[:, at], (8, width)))
        beta[...] += jnp.dot(
            jnp.concatenate([r_hi, r_lo], axis=0), both, preferred_element_type=F32
        )

    def accumulate(offs, width, first, count):
        tile = min(TILE, count)
        ats = [pl.ds(pl.multiple_of(off, width), width) for off in offs]
        for t in range(count // tile):
            block = pl.ds(first + t * tile, tile)
            hi, lo = split(jnp.concatenate([j_ref[block, at] for at in ats], axis=1))
            both = jnp.dot(
                jnp.concatenate([hi, lo], axis=0),
                jnp.concatenate([vb[at, :] for at in ats], axis=0),
                preferred_element_type=F32,
            )
            jv[block, :] += both[:tile, :K] + (both[:tile, K:] + both[tile:, :K]) + both[tile:, K:]

    piped = chunk % UNIT == 0

    def work(step, p, way):
        if not piped:
            return
        offs = [granule(w, step, 0) * part for w in range(2)]
        if p == 0:
            first = pl.multiple_of(granule(way, step, 0), parts)
            absorb(whole[pl.ds(first, parts)].reshape(chunk, K), offs[way], chunk)
        half_at = {(parts // 2 - 1, 1): 0, (parts - 1, 1): 1}.get((p, way))
        if half_at is not None:
            accumulate(offs, chunk, half_at * (rows // 2), rows // 2)

    for (p, way), value in zip(order, own(0)):
        sent[way, 0, p] = value()
        reduce_copy(0, way, p).start()
    gram[...] = jnp.zeros_like(gram)
    beta[...] = jnp.zeros_like(beta)
    jv[...] = jnp.zeros_like(jv)

    def reduce_step(step, carry):
        def load_piece(at):
            j_load(step, at, pieces).start()

        values = own(step)
        for at, (p, way) in enumerate(order):
            reduce_copy(step - 1, way, p).wait_recv()
            sent[way, step, p] = values[at]() + landed[way, step - 1, p]
            reduce_copy(step, way, p).start()
            if strips < n - 1:
                pl.when(step < strips)(functools.partial(load_piece, at))
            else:
                load_piece(at)
        if strips < n - 2:
            pl.when(step <= strips)(lambda: times_residual(step - 1))
        else:
            times_residual(step - 1)
        return carry

    lax.fori_loop(1, n - 1, reduce_step, 0)

    values = own(n - 1)
    for at, (p, way) in enumerate(order):
        reduce_copy(n - 2, way, p).wait_recv()
        spot = granule(way, n - 1, p)
        whole[spot] = values[at]() + landed[way, n - 2, p]
        spread_copy(n - 1, way, p, spot).start()
        if strips == n:
            j_load(n - 1, at, pieces).start()
    load(1).start()
    for at in range(n - 2, strips):
        times_residual(at)

    def jr_copy(k, slot):
        return to_col(jr_all.at[slot], jr_all.at[slot], jr_send.at[k], jr_recv.at[slot], peers[k])

    for k in range(nc - 1):
        jr_copy(k, me).start()

    def spread_step(step, carry):
        for p, way in order:
            at = granule(way, step, p)
            spread_copy(step - 1, way, p, at).wait_recv()
            spread_copy(step, way, p, at).start()
            work(step - 1, p, way)
        return carry

    last = 2 * (n - 1)
    lax.fori_loop(n, last, spread_step, 0)

    load(1).wait()
    for (p, way), value in zip(w_order, w_own(0)):
        w_sent[way, 0, p] = value()
        w_copy(0, way, p).start()

    for p, way in order:
        spread_copy(last - 1, way, p, granule(way, last, p)).wait_recv()
        work(last - 1, p, way)
    for p, way in order:
        work(last, p, way)
    if not piped:
        per_unit = UNIT // part
        for unit in range(cols // UNIT):
            block = jnp.concatenate([whole[unit * per_unit + s] for s in range(per_unit)], axis=0)
            absorb(block, unit * UNIT, UNIT)
        for off in range(0, cols, 2 * UNIT):
            accumulate([off, off + UNIT], UNIT, 0, rows)

    gb[:K, :] = gram[:K, :K] + (gram[:K, K:] + gram[K:, :K]) + gram[K:, K:]
    gb[K:, :] = beta[:8, :K] + (beta[:8, K:] + beta[8:, :K])

    def gb_copy(k, slot):
        return to_col(gb, gb_all.at[slot], gb_send.at[k], gb_recv.at[slot], peers[k])

    def jv_copy(k, slot, owner):
        block = pl.ds(pl.multiple_of(owner * share, share), share)
        return to_col(jv.at[block], jv_land.at[slot], jv_send.at[k], jv_recv.at[slot], peers[k])

    for k in range(nc - 1):
        gb_copy(k, me).start()
    for k in range(nc - 1):
        jv_copy(k, me, peers[k]).start()

    def w_step(step):
        for (p, way), value in zip(w_order, w_own(step)):
            w_copy(step - 1, way, p).wait_recv()
            w_sent[way, step, p] = value() + w_land[way, step - 1, p]
            w_copy(step, way, p).start()

    def regularise():
        for k in range(nc - 1):
            gb_copy(k, peers[k]).wait_recv()
        gb_all[me] = gb[...]
        sums = gb_all[0]
        for slot in range(1, nc):
            sums = sums + gb_all[slot]
        beta_ref[...] = sums[K:]
        total = sums[:K]
        trace = jnp.sum(jnp.sum(total * eye, axis=0, keepdims=True), axis=1, keepdims=True)
        regular = total + REG * (trace / K) * eye
        norm_one = jnp.max(
            jnp.sum(jnp.abs(regular), axis=0, keepdims=True), axis=1, keepdims=True
        )
        return regular, regular / (norm_one * norm_one)

    eye = (
        lax.broadcasted_iota(jnp.int32, (K, K), 0) == lax.broadcasted_iota(jnp.int32, (K, K), 1)
    ).astype(F32)
    begin = min(2, n - 2)
    for step in range(1, n - 1):
        w_step(step)
        if step == begin:
            regular, zmat = regularise()
            sweeps = 0
        if step >= begin:
            until = NS if step == n - 2 else min(NS, step - begin + 1)
            for sweep in range(sweeps, until):
                inner = jnp.dot(regular, zmat, precision=HIGH, preferred_element_type=F32)
                zmat = jnp.dot(
                    zmat, 2.0 * eye - inner, precision=HIGH, preferred_element_type=F32
                )
            sweeps = until

    for k in range(nc - 1):
        jv_copy(k, peers[k], me).wait_recv()
    jv_land[me] = jv[pl.ds(pl.multiple_of(me * share, share), share), :]
    total = jv_land[0]
    for slot in range(1, nc):
        total = total + jv_land[slot]
    jv_sum[...] = total

    for k in range(nc - 1):
        jr_copy(k, peers[k]).wait_recv()
    jr_sum = jr_all[0]
    for slot in range(1, nc):
        jr_sum = jr_sum + jr_all[slot]
    jr_ref[...] = jr_sum

    partner = me + 1 - 2 * (me % 2)
    half = nc // 2

    def u_copy(slot, hop, at, peer):
        block = u_ref.at[slot, pl.ds(at * grain, grain)]
        return to_col(block, block, u_send.at[hop, at], u_recv.at[slot, at], peer)

    z_hi, z_lo = split(zmat)
    z_both = jnp.concatenate([z_hi, z_lo], axis=1)
    values = w_own(n - 1)
    for p in range(w_parts):
        ats = [way * w_parts + p for way in range(2)]
        diffs = []
        for way in range(2):
            w_copy(n - 2, way, p).wait_recv()
            block = pl.ds(ats[way] * grain, grain)
            diffs.append(values[2 * p + way]() + w_land[way, n - 2, p] - jv_sum[block, :])
        d_hi, d_lo = split(jnp.concatenate(diffs, axis=0))
        both = jnp.dot(
            jnp.concatenate([d_hi, d_lo], axis=0), z_both, preferred_element_type=F32
        )
        size = 2 * grain
        u = both[:size, :K] + (both[:size, K:] + both[size:, :K]) + both[size:, K:]
        for way in range(2):
            at = ats[way]
            u_ref[me, pl.ds(at * grain, grain)] = u[way * grain : (way + 1) * grain]
            for k in range(1, half):
                u_copy(me, k - 1, at, (me + 2 * k) % nc).start()
            u_copy(me, half - 1, at, partner).start()
    for p, way in w_order:
        at = way * w_parts + p
        for k in range(1, half):
            slot = (me + 2 * k) % nc
            u_copy(slot, half - 1 + k, at, partner).wait_recv()
            u_copy(slot, half - 1 + k, at, partner).start()
    for p, way in w_order:
        at = way * w_parts + p
        for k in range(half):
            u_copy((partner + 2 * k) % nc, 0, at, partner).wait_recv()

    for p, way in w_order:
        for hop in range(nc - 1):
            u_copy(me, hop, way * w_parts + p, partner).wait_send()
    for k in range(nc - 1):
        gb_copy(k, me).wait_send()
        jr_copy(k, me).wait_send()
        jv_copy(k, me, peers[k]).wait_send()

    def drain(step, carry):
        for p, way in order:
            reduce_copy(step, way, p).wait_send()
            spread_copy(step + n - 1, way, p, granule(way, 0, p)).wait_send()
        for p, way in w_order:
            w_copy(step, way, p).wait_send()
        return carry

    lax.fori_loop(0, n - 1, drain, 0)


def gather(face_dof, counts, diff_inputs, diff_outputs, jacobian, residual, n, nc):
    rows, cols = jacobian.shape
    chunk = cols // (2 * n)
    part = min(PART, chunk)
    parts = chunk // part
    share = rows // nc
    grain = min(PART, share // 2)
    w_parts = share // (2 * grain)
    strips = min(n, rows // UNIT)
    runs = diff_inputs.shape[0]
    dma = pltpu.SemaphoreType.DMA
    v = pltpu.VMEM
    return pl.pallas_call(
        functools.partial(gather_kernel, n, nc, parts, w_parts),
        out_shape=(
            v((rows, cols), F32),
            v((2 * K, cols), BF16),
            v((nc, share, K), F32),
            v((8, K), F32),
            v((strips, rows // strips), F32),
        ),
        in_specs=[SMEM_SPEC] * 2 + [ANY_SPEC] * 3 + [VMEM_SPEC],
        out_specs=(VMEM_SPEC,) * 5,
        scratch_shapes=[
            pltpu.SMEM((runs // UNIT,), jnp.int32),
            v((runs // part, part, K), F32),
            v((runs // grain, grain, K), F32),
            v((cols // part, part, K), F32),
            v((2, n - 1, parts, part, K), F32),
            v((2, n - 1, parts, part, K), F32),
            v((cols, 2 * K), BF16),
            v((2 * K, 2 * K), F32),
            v((16, 2 * K), F32),
            v((rows, K), F32),
            v((2, n - 1, w_parts, grain, K), F32),
            v((2, n - 1, w_parts, grain, K), F32),
            v((nc, share, K), F32),
            v((share, K), F32),
            v((nc, strips, rows // strips), F32),
            v((K + 8, K), F32),
            v((nc, K + 8, K), F32),
            dma((2,)), dma((strips,)),
            dma((2, 2 * (n - 1), parts)), dma((2, 2 * (n - 1), parts)),
            dma((2, n - 1, w_parts)), dma((2, n - 1, w_parts)),
            dma((nc - 1,)), dma((nc,)), dma((nc - 1,)), dma((nc,)),
            dma((nc - 1,)), dma((nc,)),
            dma((nc - 1, share // grain)), dma((nc, share // grain)),
        ],
        compiler_params=pltpu.CompilerParams(
            collective_id=0, has_side_effects=True, vmem_limit_bytes=VMEM_LIMIT
        ),
    )(
        face_dof, counts,
        diff_inputs.reshape(-1, part, K), diff_outputs.reshape(-1, grain, K), jacobian, residual,
    )


def update_kernel(
    j_ref, vt_ref, u_ref, beta_ref, jr_ref, trial_ref, out_ref, corrected_ref,
    twice, low, stage, sem,
):
    rows, cols = j_ref.shape
    slots, _, width = stage.shape
    hi, lo = split(u_ref[...])
    twice[:, :K] = hi
    twice[:, K:] = hi
    low[...] = lo

    def copy(at):
        columns = pl.ds(pl.multiple_of(at * width, width), width)
        slot = at % slots
        return pltpu.make_async_copy(stage.at[slot], out_ref.at[:, columns], sem.at[slot])

    def step(at, carry):
        pl.when(at >= slots)(lambda: copy(at - slots).wait())
        columns = pl.ds(pl.multiple_of(at * width, width), width)
        main = jnp.dot(twice[...], vt_ref[:, columns], preferred_element_type=F32)
        rest = jnp.dot(low[...], vt_ref[:K, columns], preferred_element_type=F32)
        stage[at % slots] = j_ref[:, columns] + (main + rest)
        copy(at).start()
        return carry

    count = cols // width
    lax.fori_loop(0, count, step, 0)
    low_rank = jnp.sum(jnp.transpose(u_ref[...] * beta_ref[:1]), axis=0, keepdims=True)
    size = jr_ref.shape[1]
    for at in range(jr_ref.shape[0]):
        block = slice(at * size, (at + 1) * size)
        corrected_ref[:, block] = trial_ref[:, block] - (jr_ref[at : at + 1, :] + low_rank[:, block])
    for at in range(count - slots, count):
        copy(at).wait()


def update(jacobian, vt, u, beta, j_r, trial):
    rows, cols = jacobian.shape
    held = [pltpu.with_memory_space_constraint(x, pltpu.VMEM) for x in (jacobian, vt, u, beta, j_r)]
    slots = 3
    return pl.pallas_call(
        update_kernel,
        out_shape=(
            jax.ShapeDtypeStruct((rows, cols), F32),
            jax.ShapeDtypeStruct((1, rows), F32),
        ),
        in_specs=[VMEM_SPEC] * 6,
        out_specs=(ANY_SPEC, VMEM_SPEC),
        scratch_shapes=[
            pltpu.VMEM((rows, 2 * K), BF16),
            pltpu.VMEM((rows, K), BF16),
            pltpu.VMEM((slots, rows, WIDTH), F32),
            pltpu.SemaphoreType.DMA((slots,)),
        ],
        compiler_params=pltpu.CompilerParams(vmem_limit_bytes=VMEM_LIMIT),
    )(*held, trial)


def per_device(jacobian, diff_inputs, diff_outputs, face_dof, counts, residual, trial):
    row_block, col_block = jacobian.shape
    held, vt, u, beta, j_r = gather(
        face_dof, counts, diff_inputs, diff_outputs, jacobian,
        residual.reshape(1, col_block), lax.axis_size("row"), lax.axis_size("col"),
    )
    updated, corrected = update(
        held, vt, u.reshape(row_block, K), beta, j_r, trial.reshape(1, row_block)
    )
    return (updated, corrected[0])


def solution(mesh):
    placed = (
        P("row", "col"),
        P("row", None),
        P("row", None),
        P("row"),
        P("row"),
        P("col"),
        P("row"),
    )
    return jax.shard_map(
        per_device,
        mesh=mesh,
        in_specs=placed,
        out_specs=(P("row", "col"), P("row")),
        check_vma=False,
    )
```

```python
import functools

import jax
import jax.numpy as jnp
from jax import lax
from jax.experimental import pallas as pl
from jax.experimental.pallas import tpu as pltpu
from jax.sharding import PartitionSpec as P

K = 128
NS = 4
UNIT = 128
PART = 64
TILE = 1024
WIDTH = 512
VMEM_LIMIT = 26 * 2**20

HIGH = lax.Precision.HIGHEST
REG = 0.1
F32 = jnp.float32
BF16 = jnp.bfloat16
MESH = pl.DeviceIdType.MESH
VMEM_SPEC = pl.BlockSpec(memory_space=pltpu.VMEM)
ANY_SPEC = pl.BlockSpec(memory_space=pl.ANY)


def split(x):
    hi = x.astype(BF16)
    return hi, (x - hi.astype(F32)).astype(BF16)


def ring_place(index, n):
    return index // 2 + (index % 2) * (n - 1 - 2 * (index // 2))


def ring_index(place, n):
    side = place // (n // 2)
    level = place + side * (n - 1 - 2 * place)
    return 2 * level + side


def gather_kernel(
    n, nc, parts, w_parts, dof_hbm, count_hbm, v_hbm, w_hbm, j_hbm, r_hbm,
    j_ref, vt_ref, u_ref, beta_ref, jr_ref,
    dof_ref, count_ref, run_unit, r_ref, xv, xw, whole, landed, sent, vb, gram, beta, jv,
    w_land, w_sent, jv_land, jv_sum, jr_all, gb, gb_all,
    load_sem, j_sem, v_send, v_recv, w_send, w_recv,
    jv_send, jv_recv, gb_send, gb_recv, jr_send, jr_recv, u_send, u_recv,
):
    rows, cols = j_ref.shape
    part = whole.shape[1]
    chunk = part * parts
    grain = w_land.shape[3]
    share = jv_land.shape[1]
    strips, j_rows = jr_ref.shape
    me = lax.axis_index("col")
    place = ring_place(lax.axis_index("row"), n)
    right = ring_index((place + 1) % n, n)
    left = ring_index((place + n - 1) % n, n)
    peers = [(me + k) % nc for k in range(1, nc)]

    def load(k):
        source = (v_hbm, w_hbm, dof_hbm, count_hbm, r_hbm)[k]
        return pltpu.make_async_copy(
            source, (xv, xw, dof_ref, count_ref, r_ref)[k], load_sem.at[k]
        )

    pieces = 2 * parts

    def j_load(at, piece=0, count=1):
        size = j_rows // count
        block = pl.ds(pl.multiple_of(at * j_rows + piece * size, size), size)
        return pltpu.make_async_copy(j_hbm.at[block], j_ref.at[block], j_sem.at[at])

    for k in (2, 3, 0, 4):
        load(k).start()

    barrier = pltpu.get_barrier_semaphore()
    for peer in (left, right):
        pl.semaphore_signal(barrier, inc=1, device_id={"row": peer}, device_id_type=MESH)
    for peer in peers:
        pl.semaphore_signal(barrier, inc=1, device_id={"col": peer}, device_id_type=MESH)
    runs = run_unit.shape[0]
    load(2).wait()
    load(3).wait()
    for at in range(runs):
        unit = lax.shift_right_logical(dof_ref[at * UNIT], UNIT.bit_length() - 1)
        run_unit[at] = jnp.where(at * UNIT < count_ref[0], unit, -1)
    load(0).wait()
    load(4).wait()
    j_load(0).start()
    pl.semaphore_wait(barrier, 2 + len(peers))

    def to_row(source, target, send, recv, way):
        return pltpu.make_async_remote_copy(
            src_ref=source, dst_ref=target, send_sem=send, recv_sem=recv,
            device_id={"row": right if way == 0 else left}, device_id_type=MESH,
        )

    def to_col(source, target, send, recv, peer):
        return pltpu.make_async_remote_copy(
            src_ref=source, dst_ref=target, send_sem=send, recv_sem=recv,
            device_id={"col": peer}, device_id_type=MESH,
        )

    order = [(p, way) for p in range(parts) for way in range(2)]

    def granule(way, back, p):
        sign = 1 if way == 0 else -1
        at = (place + 2 * n - sign * back) % n
        return (way * n + at) * parts + p

    def locate(unit):
        src = jnp.int32(-1)
        for at in range(runs):
            src = jnp.where(run_unit[at] == unit, at, src)
        return jnp.maximum(src, 0), (src >= 0).astype(F32)

    def pick(source, rows_at):
        size = source.shape[1]
        per_unit = UNIT // size
        found, values = {}, []
        for at, same in rows_at:
            if same is None or same not in found:
                found[same] = locate(at // per_unit)
            src, mask = found[same]
            values.append(lambda src=src, mask=mask, at=at: source[src * per_unit + at % per_unit] * mask)
        return values

    def sharing(p, way, count, size):
        per_unit = UNIT // size
        return (way, p // per_unit) if count % per_unit == 0 else None

    def own(step):
        base = me * (cols // part)
        return pick(
            xv, [(base + granule(way, step, p), sharing(p, way, parts, part)) for p, way in order]
        )

    def reduce_copy(step, way, p):
        return to_row(
            sent.at[way, step, p], landed.at[way, step, p],
            v_send.at[way, step, p], v_recv.at[way, step, p], way,
        )

    def spread_copy(step, way, p, at):
        return to_row(
            whole.at[at], whole.at[at], v_send.at[way, step, p], v_recv.at[way, step, p], way
        )

    def w_copy(step, way, p):
        return to_row(
            w_sent.at[way, step, p], w_land.at[way, step, p],
            w_send.at[way, step, p], w_recv.at[way, step, p], way,
        )

    w_order = [(p, way) for p in range(w_parts) for way in range(2)]

    def w_own(step, some):
        wanted = []
        for p, way in some:
            sign = 1 if way == 0 else -1
            block = ring_index((place + 2 * n - sign * (step + 1)) % n, n)
            at = (block * rows + me * share) // grain + way * w_parts + p
            wanted.append((at, sharing(p, way, w_parts, grain)))
        return pick(xw, wanted)

    def times_residual(at):
        j_load(at).wait()
        strip = min(64, j_rows)
        sums = []
        for sub in range(j_rows // strip):
            block = pl.ds(pl.multiple_of(at * j_rows + sub * strip, strip), strip)
            total = jnp.zeros((strip, K), F32)
            for c in range(0, cols, K):
                total = total + j_ref[block, c : c + K] * r_ref[:, c : c + K]
            sums.append(total)
        total = jnp.concatenate(sums, axis=0)
        jr_all[me, pl.ds(at, 1), :] = jnp.sum(jnp.transpose(total), axis=0, keepdims=True)

    def absorb(block, off, width):
        at = pl.ds(pl.multiple_of(off, width), width)
        hi, lo = split(block)
        both = jnp.concatenate([hi, lo], axis=1)
        vb[at, :] = both
        t_hi, t_lo = split(jnp.transpose(block))
        vt_ref[:K, at] = t_hi
        vt_ref[K:, at] = t_lo
        gram[...] += lax.dot_general(
            both, both, (((0,), (0,)), ((), ())), preferred_element_type=F32
        )
        r_hi, r_lo = split(jnp.broadcast_to(r_ref[:, at], (8, width)))
        beta[...] += jnp.dot(
            jnp.concatenate([r_hi, r_lo], axis=0), both, preferred_element_type=F32
        )

    def accumulate(offs, width, first, count):
        tile = min(TILE, count)
        ats = [pl.ds(pl.multiple_of(off, width), width) for off in offs]
        for t in range(count // tile):
            block = pl.ds(first + t * tile, tile)
            hi, lo = split(jnp.concatenate([j_ref[block, at] for at in ats], axis=1))
            both = jnp.dot(
                jnp.concatenate([hi, lo], axis=0),
                jnp.concatenate([vb[at, :] for at in ats], axis=0),
                preferred_element_type=F32,
            )
            jv[block, :] += both[:tile, :K] + (both[:tile, K:] + both[tile:, :K]) + both[tile:, K:]

    piped = chunk % UNIT == 0

    def work(step, p, way):
        if not piped:
            return
        offs = [granule(w, step, 0) * part for w in range(2)]
        if p == 0:
            first = pl.multiple_of(granule(way, step, 0), parts)
            absorb(whole[pl.ds(first, parts)].reshape(chunk, K), offs[way], chunk)
        half_at = {(parts // 2 - 1, 1): 0, (parts - 1, 1): 1}.get((p, way))
        if half_at is not None:
            accumulate(offs, chunk, half_at * (rows // 2), rows // 2)

    for (p, way), value in zip(order, own(0)):
        sent[way, 0, p] = value()
        reduce_copy(0, way, p).start()
    gram[...] = jnp.zeros_like(gram)
    beta[...] = jnp.zeros_like(beta)
    jv[...] = jnp.zeros_like(jv)

    def reduce_step(step, carry):
        def load_piece(at):
            j_load(step, at, pieces).start()

        values = own(step)
        for at, (p, way) in enumerate(order):
            reduce_copy(step - 1, way, p).wait_recv()
            sent[way, step, p] = values[at]() + landed[way, step - 1, p]
            reduce_copy(step, way, p).start()
            if strips < n - 1:
                pl.when(step < strips)(functools.partial(load_piece, at))
            else:
                load_piece(at)
        if strips < n - 2:
            pl.when(step <= strips)(lambda: times_residual(step - 1))
        else:
            times_residual(step - 1)
        return carry

    lax.fori_loop(1, n - 1, reduce_step, 0)

    values = own(n - 1)
    for at, (p, way) in enumerate(order):
        reduce_copy(n - 2, way, p).wait_recv()
        spot = granule(way, n - 1, p)
        whole[spot] = values[at]() + landed[way, n - 2, p]
        spread_copy(n - 1, way, p, spot).start()
        if strips == n:
            j_load(n - 1, at, pieces).start()
    load(1).start()
    for at in range(n - 2, strips):
        times_residual(at)

    def jr_copy(k, slot):
        return to_col(jr_all.at[slot], jr_all.at[slot], jr_send.at[k], jr_recv.at[slot], peers[k])

    for k in range(nc - 1):
        jr_copy(k, me).start()

    def spread_step(step, carry):
        for p, way in order:
            at = granule(way, step, p)
            spread_copy(step - 1, way, p, at).wait_recv()
            spread_copy(step, way, p, at).start()
            reduce_copy(step - n, way, p).wait_send()
            work(step - 1, p, way)
        return carry

    last = 2 * (n - 1)
    lax.fori_loop(n, last - 1, spread_step, 0)

    def w_step(step):
        for (p, way), value in zip(w_order, w_own(step, w_order)):
            if step == 0:
                w_sent[way, 0, p] = value()
            else:
                w_copy(step - 1, way, p).wait_recv()
                w_sent[way, step, p] = value() + w_land[way, step - 1, p]
            w_copy(step, way, p).start()
        for p, way in order:
            if step > 0:
                spread_copy(n + step - 2, way, p, granule(way, 0, p)).wait_send()
        for p, way in w_order:
            if step > 1:
                w_copy(step - 2, way, p).wait_send()

    load(1).wait()
    w_step(0)
    spread_step(last - 1, 0)
    w_step(1)
    for p, way in order:
        spread_copy(last - 1, way, p, granule(way, last, p)).wait_recv()
        work(last - 1, p, way)
    w_step(2)
    for p, way in order:
        work(last, p, way)
    if not piped:
        per_unit = UNIT // part
        for unit in range(cols // UNIT):
            block = jnp.concatenate([whole[unit * per_unit + s] for s in range(per_unit)], axis=0)
            absorb(block, unit * UNIT, UNIT)
        for off in range(0, cols, 2 * UNIT):
            accumulate([off, off + UNIT], UNIT, 0, rows)

    gb[:K, :] = gram[:K, :K] + (gram[:K, K:] + gram[K:, :K]) + gram[K:, K:]
    gb[K:, :] = beta[:8, :K] + (beta[:8, K:] + beta[8:, :K])

    def gb_copy(k, slot):
        return to_col(gb, gb_all.at[slot], gb_send.at[k], gb_recv.at[slot], peers[k])

    def jv_copy(k, slot, owner):
        block = pl.ds(pl.multiple_of(owner * share, share), share)
        return to_col(jv.at[block], jv_land.at[slot], jv_send.at[k], jv_recv.at[slot], peers[k])

    for k in range(nc - 1):
        gb_copy(k, me).start()
    for k in range(nc - 1):
        jv_copy(k, me, peers[k]).start()

    def regularise():
        for k in range(nc - 1):
            gb_copy(k, peers[k]).wait_recv()
        gb_all[me] = gb[...]
        sums = gb_all[0]
        for slot in range(1, nc):
            sums = sums + gb_all[slot]
        beta_ref[...] = sums[K:]
        total = sums[:K]
        trace = jnp.sum(jnp.sum(total * eye, axis=0, keepdims=True), axis=1, keepdims=True)
        regular = total + REG * (trace / K) * eye
        norm_one = jnp.max(
            jnp.sum(jnp.abs(regular), axis=0, keepdims=True), axis=1, keepdims=True
        )
        return regular, regular / (norm_one * norm_one)

    eye = (
        lax.broadcasted_iota(jnp.int32, (K, K), 0) == lax.broadcasted_iota(jnp.int32, (K, K), 1)
    ).astype(F32)
    sweeps = 0
    for step in range(2, n - 2):
        w_step(step + 1)
        if step == 2:
            regular, zmat = regularise()
        until = NS if step == n - 3 else min(NS, step - 1)
        for sweep in range(sweeps, until):
            inner = jnp.dot(regular, zmat, precision=HIGH, preferred_element_type=F32)
            zmat = jnp.dot(zmat, 2.0 * eye - inner, precision=HIGH, preferred_element_type=F32)
        sweeps = until

    for k in range(nc - 1):
        jv_copy(k, peers[k], me).wait_recv()
    jv_land[me] = jv[pl.ds(pl.multiple_of(me * share, share), share), :]
    total = jv_land[0]
    for slot in range(1, nc):
        total = total + jv_land[slot]
    jv_sum[...] = total

    for k in range(nc - 1):
        jr_copy(k, peers[k]).wait_recv()
    jr_sum = jr_all[0]
    for slot in range(1, nc):
        jr_sum = jr_sum + jr_all[slot]
    jr_ref[...] = jr_sum

    partner = me + 1 - 2 * (me % 2)
    half = nc // 2

    def u_copy(slot, hop, at, peer):
        block = u_ref.at[slot, pl.ds(at * grain, grain)]
        return to_col(block, block, u_send.at[hop, at], u_recv.at[slot, at], peer)

    z_hi, z_lo = split(zmat)
    z_both = jnp.concatenate([z_hi, z_lo], axis=1)

    def finish(some):
        values = dict(zip(some, w_own(n - 1, some)))
        for p in sorted({p for p, way in some}):
            ats = [way * w_parts + p for way in range(2)]
            diffs = []
            for way in range(2):
                w_copy(n - 2, way, p).wait_recv()
                block = pl.ds(ats[way] * grain, grain)
                diffs.append(values[p, way]() + w_land[way, n - 2, p] - jv_sum[block, :])
            d_hi, d_lo = split(jnp.concatenate(diffs, axis=0))
            both = jnp.dot(
                jnp.concatenate([d_hi, d_lo], axis=0), z_both, preferred_element_type=F32
            )
            size = 2 * grain
            u = both[:size, :K] + (both[:size, K:] + both[size:, :K]) + both[size:, K:]
            for way in range(2):
                at = ats[way]
                u_ref[me, pl.ds(at * grain, grain)] = u[way * grain : (way + 1) * grain]
                for k in range(1, half):
                    u_copy(me, k - 1, at, (me + 2 * k) % nc).start()
                u_copy(me, half - 1, at, partner).start()

    for p, way in order:
        reduce_copy(n - 2, way, p).wait_send()
        spread_copy(last - 1, way, p, granule(way, 0, p)).wait_send()
    for p, way in w_order:
        w_copy(n - 3, way, p).wait_send()
    for k in range(nc - 1):
        gb_copy(k, me).wait_send()
        jr_copy(k, me).wait_send()
        jv_copy(k, me, peers[k]).wait_send()

    finish(w_order)
    for p, way in w_order:
        at = way * w_parts + p
        for k in range(1, half):
            slot = (me + 2 * k) % nc
            u_copy(slot, half - 1 + k, at, partner).wait_recv()
            u_copy(slot, half - 1 + k, at, partner).start()
    for p, way in w_order:
        at = way * w_parts + p
        for k in range(half):
            u_copy((partner + 2 * k) % nc, 0, at, partner).wait_recv()

    for p, way in w_order:
        for hop in range(nc - 1):
            u_copy(me, hop, way * w_parts + p, partner).wait_send()
    for p, way in w_order:
        w_copy(n - 2, way, p).wait_send()


def gather(face_dof, counts, diff_inputs, diff_outputs, jacobian, residual, n, nc):
    rows, cols = jacobian.shape
    chunk = cols // (2 * n)
    part = min(PART, chunk)
    parts = chunk // part
    share = rows // nc
    grain = min(PART, share // 2)
    w_parts = share // (2 * grain)
    strips = min(n, rows // UNIT)
    runs = diff_inputs.shape[0]
    dma = pltpu.SemaphoreType.DMA
    v = pltpu.VMEM
    return pl.pallas_call(
        functools.partial(gather_kernel, n, nc, parts, w_parts),
        out_shape=(
            v((rows, cols), F32),
            v((2 * K, cols), BF16),
            v((nc, share, K), F32),
            v((8, K), F32),
            v((strips, rows // strips), F32),
        ),
        in_specs=[ANY_SPEC] * 6,
        out_specs=(VMEM_SPEC,) * 5,
        scratch_shapes=[
            pltpu.SMEM((runs,), jnp.int32),
            pltpu.SMEM((1,), jnp.int32),
            pltpu.SMEM((runs // UNIT,), jnp.int32),
            v((1, cols), F32),
            v((runs // part, part, K), F32),
            v((runs // grain, grain, K), F32),
            v((cols // part, part, K), F32),
            v((2, n - 1, parts, part, K), F32),
            v((2, n - 1, parts, part, K), F32),
            v((cols, 2 * K), BF16),
            v((2 * K, 2 * K), F32),
            v((16, 2 * K), F32),
            v((rows, K), F32),
            v((2, n - 1, w_parts, grain, K), F32),
            v((2, n - 1, w_parts, grain, K), F32),
            v((nc, share, K), F32),
            v((share, K), F32),
            v((nc, strips, rows // strips), F32),
            v((K + 8, K), F32),
            v((nc, K + 8, K), F32),
            dma((5,)), dma((strips,)),
            dma((2, 2 * (n - 1), parts)), dma((2, 2 * (n - 1), parts)),
            dma((2, n - 1, w_parts)), dma((2, n - 1, w_parts)),
            dma((nc - 1,)), dma((nc,)), dma((nc - 1,)), dma((nc,)),
            dma((nc - 1,)), dma((nc,)),
            dma((nc - 1, share // grain)), dma((nc, share // grain)),
        ],
        compiler_params=pltpu.CompilerParams(
            collective_id=0, has_side_effects=True, vmem_limit_bytes=VMEM_LIMIT
        ),
    )(
        face_dof, counts,
        diff_inputs.reshape(-1, part, K), diff_outputs.reshape(-1, grain, K), jacobian, residual,
    )


def update_kernel(
    j_ref, vt_ref, u_ref, beta_ref, jr_ref, trial_ref, out_ref, corrected_ref,
    twice, low, stage, sem,
):
    rows, cols = j_ref.shape
    slots, _, width = stage.shape
    hi, lo = split(u_ref[...])
    twice[:, :K] = hi
    twice[:, K:] = hi
    low[...] = lo

    def copy(at):
        columns = pl.ds(pl.multiple_of(at * width, width), width)
        slot = at % slots
        return pltpu.make_async_copy(stage.at[slot], out_ref.at[:, columns], sem.at[slot])

    def step(at, carry):
        pl.when(at >= slots)(lambda: copy(at - slots).wait())
        columns = pl.ds(pl.multiple_of(at * width, width), width)
        main = jnp.dot(twice[...], vt_ref[:, columns], preferred_element_type=F32)
        rest = jnp.dot(low[...], vt_ref[:K, columns], preferred_element_type=F32)
        stage[at % slots] = j_ref[:, columns] + (main + rest)
        copy(at).start()
        return carry

    count = cols // width
    lax.fori_loop(0, count, step, 0)
    low_rank = jnp.sum(jnp.transpose(u_ref[...] * beta_ref[:1]), axis=0, keepdims=True)
    size = jr_ref.shape[1]
    for at in range(jr_ref.shape[0]):
        block = slice(at * size, (at + 1) * size)
        corrected_ref[:, block] = trial_ref[:, block] - (jr_ref[at : at + 1, :] + low_rank[:, block])
    for at in range(count - slots, count):
        copy(at).wait()


def update(jacobian, vt, u, beta, j_r, trial):
    rows, cols = jacobian.shape
    held = [pltpu.with_memory_space_constraint(x, pltpu.VMEM) for x in (jacobian, vt, u, beta, j_r)]
    slots = 3
    return pl.pallas_call(
        update_kernel,
        out_shape=(
            jax.ShapeDtypeStruct((rows, cols), F32),
            jax.ShapeDtypeStruct((1, rows), F32),
        ),
        in_specs=[VMEM_SPEC] * 6,
        out_specs=(ANY_SPEC, VMEM_SPEC),
        scratch_shapes=[
            pltpu.VMEM((rows, 2 * K), BF16),
            pltpu.VMEM((rows, K), BF16),
            pltpu.VMEM((slots, rows, WIDTH), F32),
            pltpu.SemaphoreType.DMA((slots,)),
        ],
        compiler_params=pltpu.CompilerParams(vmem_limit_bytes=VMEM_LIMIT),
    )(*held, trial)


def per_device(jacobian, diff_inputs, diff_outputs, face_dof, counts, residual, trial):
    row_block, col_block = jacobian.shape
    held, vt, u, beta, j_r = gather(
        face_dof, counts, diff_inputs, diff_outputs, jacobian,
        residual.reshape(1, col_block), lax.axis_size("row"), lax.axis_size("col"),
    )
    updated, corrected = update(
        held, vt, u.reshape(row_block, K), beta, j_r, trial.reshape(1, row_block)
    )
    return (updated, corrected[0])


def solution(mesh):
    placed = (
        P("row", "col"),
        P("row", None),
        P("row", None),
        P("row"),
        P("row"),
        P("col"),
        P("row"),
    )
    return jax.shard_map(
        per_device,
        mesh=mesh,
        in_specs=placed,
        out_specs=(P("row", "col"), P("row")),
        check_vma=False,
    )
```

```python
import functools

import jax
import jax.numpy as jnp
from jax import lax
from jax.experimental import pallas as pl
from jax.experimental.pallas import tpu as pltpu
from jax.sharding import PartitionSpec as P

K = 128
NS = 4
UNIT = 128
PART = 64
TILE = 1024
WIDTH = 512
VMEM_LIMIT = 26 * 2**20

HIGH = lax.Precision.HIGHEST
REG = 0.1
F32 = jnp.float32
BF16 = jnp.bfloat16
MESH = pl.DeviceIdType.MESH
VMEM_SPEC = pl.BlockSpec(memory_space=pltpu.VMEM)
ANY_SPEC = pl.BlockSpec(memory_space=pl.ANY)


def split(x):
    hi = x.astype(BF16)
    return hi, (x - hi.astype(F32)).astype(BF16)


def ring_place(index, n):
    return index // 2 + (index % 2) * (n - 1 - 2 * (index // 2))


def ring_index(place, n):
    side = place // (n // 2)
    level = place + side * (n - 1 - 2 * place)
    return 2 * level + side


def gather_kernel(
    n, nc, parts, w_parts, dof_hbm, count_hbm, v_hbm, w_hbm, j_hbm, r_hbm,
    j_ref, vt_ref, u_ref, beta_ref, jr_ref,
    dof_ref, count_ref, run_unit, r_ref, xv, xw, whole, landed, sent, vb, gram, beta, jv,
    w_land, w_sent, jv_land, jv_sum, jr_all, gb, gb_all, twice, low,
    load_sem, j_sem, v_send, v_recv, w_send, w_recv,
    jv_send, jv_recv, gb_send, gb_recv, jr_send, jr_recv, u_send, u_recv,
):
    rows, cols = j_ref.shape
    part = whole.shape[1]
    chunk = part * parts
    grain = w_land.shape[3]
    share = jv_land.shape[1]
    strips, j_rows = jr_ref.shape
    me = lax.axis_index("col")
    place = ring_place(lax.axis_index("row"), n)
    right = ring_index((place + 1) % n, n)
    left = ring_index((place + n - 1) % n, n)
    peers = [(me + k) % nc for k in range(1, nc)]

    def load(k):
        source = (v_hbm, w_hbm, dof_hbm, count_hbm, r_hbm)[k]
        return pltpu.make_async_copy(
            source, (xv, xw, dof_ref, count_ref, r_ref)[k], load_sem.at[k]
        )

    pieces = 2 * parts

    def j_load(at, piece=0, count=1):
        size = j_rows // count
        block = pl.ds(pl.multiple_of(at * j_rows + piece * size, size), size)
        return pltpu.make_async_copy(j_hbm.at[block], j_ref.at[block], j_sem.at[at])

    for k in (2, 3, 0, 4):
        load(k).start()

    barrier = pltpu.get_barrier_semaphore()
    for peer in (left, right):
        pl.semaphore_signal(barrier, inc=1, device_id={"row": peer}, device_id_type=MESH)
    for peer in peers:
        pl.semaphore_signal(barrier, inc=1, device_id={"col": peer}, device_id_type=MESH)
    runs = run_unit.shape[0]
    load(2).wait()
    load(3).wait()
    for at in range(runs):
        unit = lax.shift_right_logical(dof_ref[at * UNIT], UNIT.bit_length() - 1)
        run_unit[at] = jnp.where(at * UNIT < count_ref[0], unit, -1)
    load(0).wait()
    load(4).wait()
    j_load(0).start()
    pl.semaphore_wait(barrier, 2 + len(peers))

    def to_row(source, target, send, recv, way):
        return pltpu.make_async_remote_copy(
            src_ref=source, dst_ref=target, send_sem=send, recv_sem=recv,
            device_id={"row": right if way == 0 else left}, device_id_type=MESH,
        )

    def to_col(source, target, send, recv, peer):
        return pltpu.make_async_remote_copy(
            src_ref=source, dst_ref=target, send_sem=send, recv_sem=recv,
            device_id={"col": peer}, device_id_type=MESH,
        )

    order = [(p, way) for p in range(parts) for way in range(2)]

    def granule(way, back, p):
        sign = 1 if way == 0 else -1
        at = (place + 2 * n - sign * back) % n
        return (way * n + at) * parts + p

    def locate(unit):
        src = jnp.int32(-1)
        for at in range(runs):
            src = jnp.where(run_unit[at] == unit, at, src)
        return jnp.maximum(src, 0), (src >= 0).astype(F32)

    def pick(source, rows_at):
        size = source.shape[1]
        per_unit = UNIT // size
        found, values = {}, []
        for at, same in rows_at:
            if same is None or same not in found:
                found[same] = locate(at // per_unit)
            src, mask = found[same]
            values.append(lambda src=src, mask=mask, at=at: source[src * per_unit + at % per_unit] * mask)
        return values

    def sharing(p, way, count, size):
        per_unit = UNIT // size
        return (way, p // per_unit) if count % per_unit == 0 else None

    def own(step):
        base = me * (cols // part)
        return pick(
            xv, [(base + granule(way, step, p), sharing(p, way, parts, part)) for p, way in order]
        )

    def reduce_copy(step, way, p):
        return to_row(
            sent.at[way, step, p], landed.at[way, step, p],
            v_send.at[way, step, p], v_recv.at[way, step, p], way,
        )

    def spread_copy(step, way, p, at):
        return to_row(
            whole.at[at], whole.at[at], v_send.at[way, step, p], v_recv.at[way, step, p], way
        )

    def w_copy(step, way, p):
        return to_row(
            w_sent.at[way, step, p], w_land.at[way, step, p],
            w_send.at[way, step, p], w_recv.at[way, step, p], way,
        )

    w_order = [(p, way) for p in range(w_parts) for way in range(2)]

    def w_own(step, some):
        wanted = []
        for p, way in some:
            sign = 1 if way == 0 else -1
            block = ring_index((place + 2 * n - sign * (step + 1)) % n, n)
            at = (block * rows + me * share) // grain + way * w_parts + p
            wanted.append((at, sharing(p, way, w_parts, grain)))
        return pick(xw, wanted)

    def times_residual(at):
        j_load(at).wait()
        strip = min(64, j_rows)
        sums = []
        for sub in range(j_rows // strip):
            block = pl.ds(pl.multiple_of(at * j_rows + sub * strip, strip), strip)
            total = jnp.zeros((strip, K), F32)
            for c in range(0, cols, K):
                total = total + j_ref[block, c : c + K] * r_ref[:, c : c + K]
            sums.append(total)
        total = jnp.concatenate(sums, axis=0)
        jr_all[me, pl.ds(at, 1), :] = jnp.sum(jnp.transpose(total), axis=0, keepdims=True)

    def absorb(block, off, width):
        at = pl.ds(pl.multiple_of(off, width), width)
        hi, lo = split(block)
        both = jnp.concatenate([hi, lo], axis=1)
        vb[at, :] = both
        t_hi, t_lo = split(jnp.transpose(block))
        vt_ref[:K, at] = t_hi
        vt_ref[K:, at] = t_lo
        gram[...] += lax.dot_general(
            both, both, (((0,), (0,)), ((), ())), preferred_element_type=F32
        )
        r_hi, r_lo = split(jnp.broadcast_to(r_ref[:, at], (8, width)))
        beta[...] += jnp.dot(
            jnp.concatenate([r_hi, r_lo], axis=0), both, preferred_element_type=F32
        )

    def accumulate(offs, width, first, count):
        tile = min(TILE, count)
        ats = [pl.ds(pl.multiple_of(off, width), width) for off in offs]
        for t in range(count // tile):
            block = pl.ds(first + t * tile, tile)
            hi, lo = split(jnp.concatenate([j_ref[block, at] for at in ats], axis=1))
            both = jnp.dot(
                jnp.concatenate([hi, lo], axis=0),
                jnp.concatenate([vb[at, :] for at in ats], axis=0),
                preferred_element_type=F32,
            )
            jv[block, :] += both[:tile, :K] + (both[:tile, K:] + both[tile:, :K]) + both[tile:, K:]

    piped = chunk % UNIT == 0

    def work(step, p, way):
        if not piped:
            return
        offs = [granule(w, step, 0) * part for w in range(2)]
        if p == 0:
            first = pl.multiple_of(granule(way, step, 0), parts)
            absorb(whole[pl.ds(first, parts)].reshape(chunk, K), offs[way], chunk)
        half_at = {(parts // 2 - 1, 1): 0, (parts - 1, 1): 1}.get((p, way))
        if half_at is not None:
            accumulate(offs, chunk, half_at * (rows // 2), rows // 2)

    for (p, way), value in zip(order, own(0)):
        sent[way, 0, p] = value()
        reduce_copy(0, way, p).start()
    gram[...] = jnp.zeros_like(gram)
    beta[...] = jnp.zeros_like(beta)
    jv[...] = jnp.zeros_like(jv)

    def reduce_step(step, carry):
        def load_piece(at):
            j_load(step, at, pieces).start()

        values = own(step)
        for at, (p, way) in enumerate(order):
            reduce_copy(step - 1, way, p).wait_recv()
            sent[way, step, p] = values[at]() + landed[way, step - 1, p]
            reduce_copy(step, way, p).start()
            if strips < n - 1:
                pl.when(step < strips)(functools.partial(load_piece, at))
            else:
                load_piece(at)
        if strips < n - 2:
            pl.when(step <= strips)(lambda: times_residual(step - 1))
        else:
            times_residual(step - 1)
        return carry

    lax.fori_loop(1, n - 1, reduce_step, 0)

    values = own(n - 1)
    for at, (p, way) in enumerate(order):
        reduce_copy(n - 2, way, p).wait_recv()
        spot = granule(way, n - 1, p)
        whole[spot] = values[at]() + landed[way, n - 2, p]
        spread_copy(n - 1, way, p, spot).start()
        if strips == n:
            j_load(n - 1, at, pieces).start()
    load(1).start()
    for at in range(n - 2, strips):
        times_residual(at)

    def jr_copy(k, slot):
        return to_col(jr_all.at[slot], jr_all.at[slot], jr_send.at[k], jr_recv.at[slot], peers[k])

    for k in range(nc - 1):
        jr_copy(k, me).start()

    def spread_step(step, carry):
        for p, way in order:
            at = granule(way, step, p)
            spread_copy(step - 1, way, p, at).wait_recv()
            spread_copy(step, way, p, at).start()
            reduce_copy(step - n, way, p).wait_send()
            work(step - 1, p, way)
        return carry

    last = 2 * (n - 1)
    lax.fori_loop(n, last - 1, spread_step, 0)

    def w_step(step):
        for (p, way), value in zip(w_order, w_own(step, w_order)):
            if step == 0:
                w_sent[way, 0, p] = value()
            else:
                w_copy(step - 1, way, p).wait_recv()
                w_sent[way, step, p] = value() + w_land[way, step - 1, p]
            w_copy(step, way, p).start()
        for p, way in order:
            if step > 0:
                spread_copy(n + step - 2, way, p, granule(way, 0, p)).wait_send()
        for p, way in w_order:
            if step > 1:
                w_copy(step - 2, way, p).wait_send()

    load(1).wait()
    w_step(0)
    spread_step(last - 1, 0)
    w_step(1)
    for p, way in order:
        spread_copy(last - 1, way, p, granule(way, last, p)).wait_recv()
        work(last - 1, p, way)
    w_step(2)
    for p, way in order:
        work(last, p, way)
    if not piped:
        per_unit = UNIT // part
        for unit in range(cols // UNIT):
            block = jnp.concatenate([whole[unit * per_unit + s] for s in range(per_unit)], axis=0)
            absorb(block, unit * UNIT, UNIT)
        for off in range(0, cols, 2 * UNIT):
            accumulate([off, off + UNIT], UNIT, 0, rows)

    gb[:K, :] = gram[:K, :K] + (gram[:K, K:] + gram[K:, :K]) + gram[K:, K:]
    gb[K:, :] = beta[:8, :K] + (beta[:8, K:] + beta[8:, :K])

    def gb_copy(k, slot):
        return to_col(gb, gb_all.at[slot], gb_send.at[k], gb_recv.at[slot], peers[k])

    def jv_copy(k, slot, owner):
        block = pl.ds(pl.multiple_of(owner * share, share), share)
        return to_col(jv.at[block], jv_land.at[slot], jv_send.at[k], jv_recv.at[slot], peers[k])

    for k in range(nc - 1):
        gb_copy(k, me).start()
    for k in range(nc - 1):
        jv_copy(k, me, peers[k]).start()

    def regularise():
        for k in range(nc - 1):
            gb_copy(k, peers[k]).wait_recv()
        gb_all[me] = gb[...]
        sums = gb_all[0]
        for slot in range(1, nc):
            sums = sums + gb_all[slot]
        beta_ref[...] = sums[K:]
        total = sums[:K]
        trace = jnp.sum(jnp.sum(total * eye, axis=0, keepdims=True), axis=1, keepdims=True)
        regular = total + REG * (trace / K) * eye
        norm_one = jnp.max(
            jnp.sum(jnp.abs(regular), axis=0, keepdims=True), axis=1, keepdims=True
        )
        return regular, regular / (norm_one * norm_one)

    eye = (
        lax.broadcasted_iota(jnp.int32, (K, K), 0) == lax.broadcasted_iota(jnp.int32, (K, K), 1)
    ).astype(F32)
    sweeps = 0
    for step in range(2, n - 2):
        w_step(step + 1)
        if step == 2:
            regular, zmat = regularise()
        until = NS if step == n - 3 else min(NS, step - 1)
        for sweep in range(sweeps, until):
            inner = jnp.dot(regular, zmat, precision=HIGH, preferred_element_type=F32)
            zmat = jnp.dot(zmat, 2.0 * eye - inner, precision=HIGH, preferred_element_type=F32)
        sweeps = until

    for k in range(nc - 1):
        jv_copy(k, peers[k], me).wait_recv()
    jv_land[me] = jv[pl.ds(pl.multiple_of(me * share, share), share), :]
    total = jv_land[0]
    for slot in range(1, nc):
        total = total + jv_land[slot]
    jv_sum[...] = total

    for k in range(nc - 1):
        jr_copy(k, peers[k]).wait_recv()
    jr_sum = jr_all[0]
    for slot in range(1, nc):
        jr_sum = jr_sum + jr_all[slot]
    jr_ref[...] = jr_sum

    partner = me + 1 - 2 * (me % 2)
    half = nc // 2

    def u_copy(slot, hop, at, peer):
        block = u_ref.at[slot, pl.ds(pl.multiple_of(at * grain, grain), grain)]
        return to_col(block, block, u_send.at[hop, at], u_recv.at[slot, at], peer)

    z_hi, z_lo = split(zmat)
    z_both = jnp.concatenate([z_hi, z_lo], axis=1)

    def finish(some):
        values = dict(zip(some, w_own(n - 1, some)))
        for p in sorted({p for p, way in some}):
            ats = [way * w_parts + p for way in range(2)]
            diffs = []
            for way in range(2):
                w_copy(n - 2, way, p).wait_recv()
                block = pl.ds(ats[way] * grain, grain)
                diffs.append(values[p, way]() + w_land[way, n - 2, p] - jv_sum[block, :])
            d_hi, d_lo = split(jnp.concatenate(diffs, axis=0))
            both = jnp.dot(
                jnp.concatenate([d_hi, d_lo], axis=0), z_both, preferred_element_type=F32
            )
            size = 2 * grain
            u = both[:size, :K] + (both[:size, K:] + both[size:, :K]) + both[size:, K:]
            for way in range(2):
                at = ats[way]
                u_ref[me, pl.ds(at * grain, grain)] = u[way * grain : (way + 1) * grain]
                for k in range(1, half):
                    u_copy(me, k - 1, at, (me + 2 * k) % nc).start()
                u_copy(me, half - 1, at, partner).start()

    for p, way in order:
        reduce_copy(n - 2, way, p).wait_send()
        spread_copy(last - 1, way, p, granule(way, 0, p)).wait_send()
    for p, way in w_order:
        w_copy(n - 3, way, p).wait_send()
    for k in range(nc - 1):
        gb_copy(k, me).wait_send()
        jr_copy(k, me).wait_send()
        jv_copy(k, me, peers[k]).wait_send()

    finish(w_order)
    grains = 2 * w_parts
    for at in range(grains):
        u_copy(partner, 0, at, partner).wait_recv()
    pair = me // 2
    hi, lo = split(u_ref[pl.ds(2 * pair, 2)].reshape(2 * share, K))
    twice[:, :K] = hi
    twice[:, K:] = hi
    low[...] = lo
    near = pl.ds(pl.multiple_of(pair * 2 * share, 2 * share), 2 * share)
    width = cols // grains

    def pass_on(index, carry):
        at = (index % 2) * w_parts + index // 2
        for k in range(1, half):
            slot = (me + 2 * k) % nc
            u_copy(slot, half - 1 + k, at, partner).wait_recv()
            u_copy(slot, half - 1 + k, at, partner).start()

        @pl.when(index < grains // 2)
        def _():
            columns = pl.ds(pl.multiple_of(index * width, width), width)
            main = jnp.dot(twice[...], vt_ref[:, columns], preferred_element_type=F32)
            rest = jnp.dot(low[...], vt_ref[:K, columns], preferred_element_type=F32)
            j_ref[near, columns] += main + rest

        return carry

    lax.fori_loop(0, grains, pass_on, 0)
    for at in range(grains):
        for k in range(1, half):
            u_copy((partner + 2 * k) % nc, 0, at, partner).wait_recv()

    for p, way in w_order:
        for hop in range(nc - 1):
            u_copy(me, hop, way * w_parts + p, partner).wait_send()
    for p, way in w_order:
        w_copy(n - 2, way, p).wait_send()


def gather(face_dof, counts, diff_inputs, diff_outputs, jacobian, residual, n, nc):
    rows, cols = jacobian.shape
    chunk = cols // (2 * n)
    part = min(PART, chunk)
    parts = chunk // part
    share = rows // nc
    grain = min(PART, share // 2)
    w_parts = share // (2 * grain)
    strips = min(n, rows // UNIT)
    runs = diff_inputs.shape[0]
    dma = pltpu.SemaphoreType.DMA
    v = pltpu.VMEM
    return pl.pallas_call(
        functools.partial(gather_kernel, n, nc, parts, w_parts),
        out_shape=(
            v((rows, cols), F32),
            v((2 * K, cols), BF16),
            v((nc, share, K), F32),
            v((8, K), F32),
            v((strips, rows // strips), F32),
        ),
        in_specs=[ANY_SPEC] * 6,
        out_specs=(VMEM_SPEC,) * 5,
        scratch_shapes=[
            pltpu.SMEM((runs,), jnp.int32),
            pltpu.SMEM((1,), jnp.int32),
            pltpu.SMEM((runs // UNIT,), jnp.int32),
            v((1, cols), F32),
            v((runs // part, part, K), F32),
            v((runs // grain, grain, K), F32),
            v((cols // part, part, K), F32),
            v((2, n - 1, parts, part, K), F32),
            v((2, n - 1, parts, part, K), F32),
            v((cols, 2 * K), BF16),
            v((2 * K, 2 * K), F32),
            v((16, 2 * K), F32),
            v((rows, K), F32),
            v((2, n - 1, w_parts, grain, K), F32),
            v((2, n - 1, w_parts, grain, K), F32),
            v((nc, share, K), F32),
            v((share, K), F32),
            v((nc, strips, rows // strips), F32),
            v((K + 8, K), F32),
            v((nc, K + 8, K), F32),
            v((2 * share, 2 * K), BF16),
            v((2 * share, K), BF16),
            dma((5,)), dma((strips,)),
            dma((2, 2 * (n - 1), parts)), dma((2, 2 * (n - 1), parts)),
            dma((2, n - 1, w_parts)), dma((2, n - 1, w_parts)),
            dma((nc - 1,)), dma((nc,)), dma((nc - 1,)), dma((nc,)),
            dma((nc - 1,)), dma((nc,)),
            dma((nc - 1, share // grain)), dma((nc, share // grain)),
        ],
        compiler_params=pltpu.CompilerParams(
            collective_id=0, has_side_effects=True, vmem_limit_bytes=VMEM_LIMIT
        ),
    )(
        face_dof, counts,
        diff_inputs.reshape(-1, part, K), diff_outputs.reshape(-1, grain, K), jacobian, residual,
    )


def update_kernel(
    nc, j_ref, vt_ref, u_ref, beta_ref, jr_ref, trial_hbm, out_ref, corrected_hbm,
    trial, corrected, twice, low, stage, whole_sem, stage_sem, small_sem,
):
    rows, cols = j_ref.shape
    slots, size, width = stage.shape
    pairs = nc // 2
    pair = lax.axis_index("col") // 2
    pieces = whole_sem.shape[0]
    piece = size // pieces

    def ready(at):
        block = pl.ds(pl.multiple_of(pair * size + at * piece, piece), piece)
        half = pl.ds(0, cols // 2)
        return pltpu.make_async_copy(
            j_ref.at[block, half], out_ref.at[block, half], whole_sem.at[at]
        )

    for at in range(pieces):
        ready(at).start()
    load = pltpu.make_async_copy(trial_hbm, trial, small_sem.at[0])
    load.start()
    per = cols // width
    done = per // 2
    count = per * pairs - done

    def place(at):
        at = at + done
        other = (pair + at // per) % pairs
        block = pl.ds(pl.multiple_of(other * size, size), size)
        return block, pl.ds(pl.multiple_of((at % per) * width, width), width)

    def copy(at):
        return pltpu.make_async_copy(
            stage.at[at % slots], out_ref.at[place(at)], stage_sem.at[at % slots]
        )

    def step(at, carry):
        pl.when(at >= slots)(lambda: copy(at - slots).wait())
        block, columns = place(at)

        @pl.when((at == 0) | ((at + done) % per == 0))
        def _():
            hi, lo = split(u_ref[block, :])
            twice[:, :K] = hi
            twice[:, K:] = hi
            low[...] = lo

        main = jnp.dot(twice[...], vt_ref[:, columns], preferred_element_type=F32)
        rest = jnp.dot(low[...], vt_ref[:K, columns], preferred_element_type=F32)
        stage[at % slots] = j_ref[block, columns] + (main + rest)
        copy(at).start()
        return carry

    lax.fori_loop(0, count, step, 0)
    low_rank = jnp.sum(jnp.transpose(u_ref[...] * beta_ref[:1]), axis=0, keepdims=True)
    load.wait()
    strip = jr_ref.shape[1]
    for at in range(jr_ref.shape[0]):
        block = slice(at * strip, (at + 1) * strip)
        corrected[:, block] = trial[:, block] - (jr_ref[at : at + 1, :] + low_rank[:, block])
    store = pltpu.make_async_copy(corrected, corrected_hbm, small_sem.at[1])
    store.start()
    for at in range(pieces):
        ready(at).wait()
    for at in range(max(0, count - slots), count):
        copy(at).wait()
    store.wait()


def update(jacobian, vt, u, beta, j_r, trial, nc):
    rows, cols = jacobian.shape
    held = [pltpu.with_memory_space_constraint(x, pltpu.VMEM) for x in (jacobian, vt, u, beta, j_r)]
    slots, size, pieces = 4, 2 * rows // nc, 4
    dma = pltpu.SemaphoreType.DMA
    return pl.pallas_call(
        functools.partial(update_kernel, nc),
        out_shape=(
            jax.ShapeDtypeStruct((rows, cols), F32),
            jax.ShapeDtypeStruct((1, rows), F32),
        ),
        in_specs=[VMEM_SPEC] * 5 + [ANY_SPEC],
        out_specs=(ANY_SPEC, ANY_SPEC),
        scratch_shapes=[
            pltpu.VMEM((1, rows), F32),
            pltpu.VMEM((1, rows), F32),
            pltpu.VMEM((size, 2 * K), BF16),
            pltpu.VMEM((size, K), BF16),
            pltpu.VMEM((slots, size, WIDTH), F32),
            dma((pieces,)), dma((slots,)), dma((2,)),
        ],
        compiler_params=pltpu.CompilerParams(vmem_limit_bytes=VMEM_LIMIT),
    )(*held, trial)


def per_device(jacobian, diff_inputs, diff_outputs, face_dof, counts, residual, trial):
    row_block, col_block = jacobian.shape
    held, vt, u, beta, j_r = gather(
        face_dof, counts, diff_inputs, diff_outputs, jacobian,
        residual.reshape(1, col_block), lax.axis_size("row"), lax.axis_size("col"),
    )
    updated, corrected = update(
        held, vt, u.reshape(row_block, K), beta, j_r, trial.reshape(1, row_block),
        lax.axis_size("col"),
    )
    return (updated, corrected[0])


def solution(mesh):
    placed = (
        P("row", "col"),
        P("row", None),
        P("row", None),
        P("row"),
        P("row"),
        P("col"),
        P("row"),
    )
    return jax.shard_map(
        per_device,
        mesh=mesh,
        in_specs=placed,
        out_specs=(P("row", "col"), P("row")),
        check_vma=False,
    )
```
